32 devices in a mesh: section: 4 (over x, core), dp: 8 (over z, y).
Axes of the slice: x: 2, y: 2, z: 4, core: 2. Of those that a mesh axis runs over, the one named last changes fastest.
Arguments:
- latent_states: bfloat16 [4, 32, 96, 2048], P('section', 'dp'), may hold values from -8 to 8
- rescale_factor: float32 [2048], replicated, may hold values from 0.25 to 1.75
- embedding_matrix: bfloat16 [2048, 128], P('section'), may hold values from -0.125 to 0.125
- request_span: int32 [4, 32], replicated, may hold values from 8 to 32
- passage_span: int32 [4, 32], replicated, may hold values from 32 to 64
- matching_pair: int32 [4, 32], replicated, may hold values from 0 to 31, each once within a row
- steepness_pair: float32 [2], replicated, may hold values from 8 to 400
Outputs:
- grad_hidden: bfloat16 [4, 32, 96, 2048], P('section', 'dp')
- pair_loss: float32 [4, 32], P('section', 'dp')
The draws below stay inside these ranges and needn't reach their ends.
Inputs may be any that keep to these rules, and one draw needn't show every extreme that they name: Each matching_pair[m] names every pair of the micro-batch once.
All inputs are finite; a program needn't handle non-finite values.
Results may differ from the reference program's by a relative error of at most 0.006.
The reference program's roundings to bfloat16 on the way count: a program that leaves them out, or rounds other values in their place, can miss the bound.
Values may be sent and summed in bfloat16 or wider, within the bound.
A program may use at most 64 MiB of HBM per device.

```python
import jax
import jax.numpy as jnp
from jax import lax

D = 2048
E = 128
QLEN = 32
DLEN = 64
MICRO = 4
PAIRS_ALL = 32


def draw_latent_states(key, part):
    shape = (MICRO, PAIRS_ALL, QLEN + DLEN, D)
    keys = jax.random.split(jax.random.fold_in(key, 11), 1)
    base = jnp.clip(jax.random.normal(keys[0], shape, jnp.float32), -6.0, 6.0)
    return base.astype(jnp.bfloat16)


def draw_steepness_pair(key, part):
    first_key, latter_seed = jax.random.split(jax.random.fold_in(key, 23))
    pooling_steepness = jax.random.uniform(first_key, (), jnp.float32, 8.0, 32.0)
    logit_multiplier = jax.random.uniform(latter_seed, (), jnp.float32, 10.0, 30.0)
    return jnp.stack([pooling_steepness, logit_multiplier])


def plant(result, key, smallest, high):
    spot = [jax.random.randint(jax.random.fold_in(key, axis), (), 0, length) for axis, length in enumerate(result.shape)]
    widest = result.shape.index(max(result.shape))
    next_to = spot[:widest] + [(spot[widest] + 1) % result.shape[widest]] + spot[widest + 1:]
    return result.at[tuple(spot)].set(smallest).at[tuple(next_to)].set(high)


def steps_of(stream_key, shape, cuts, smallest, largest):
    gain, own = 1.0, jax.random.fold_in(stream_key, 6)
    for axis_at, parts in cuts:
        heights = jnp.exp(jax.random.uniform(jax.random.fold_in(own, axis_at), (parts,), jnp.float32, smallest / len(cuts), largest / len(cuts)))
        gain = gain * jnp.repeat(heights, shape[axis_at] // parts).reshape([-1 if axis == axis_at else 1 for axis in range(len(shape))])
    return gain


def scatter_about(rng, shape, deviation, bound, cuts=(), kind=jnp.bfloat16):
    entries = deviation * jax.random.normal(rng, shape, jnp.float32)
    if cuts:
        entries = entries * steps_of(rng, shape, cuts, -0.22, 0.18)
    return jnp.clip(entries, -bound, bound).astype(kind)


def setup_inputs(seed: int = 0) -> dict:
    streams_of = jax.random.split(jax.random.key(seed), 8)
    return {
        "latent_states": draw_latent_states(jax.random.fold_in(streams_of[7], 71), 0),
        "rescale_factor": jnp.clip(1.0 + 0.15 * jax.random.normal(streams_of[1], (D,), jnp.float32), 0.25, 1.75),
        "embedding_matrix": scatter_about(streams_of[2], (D, E), D ** -0.5, 0.125, ((0, 4),)),
        "request_span": plant(jax.random.randint(streams_of[3], (MICRO, PAIRS_ALL), QLEN // 4, QLEN + 1), jax.random.fold_in(streams_of[3], 1), QLEN // 4, QLEN).astype(jnp.int32),
        "passage_span": plant(jax.random.randint(streams_of[4], (MICRO, PAIRS_ALL), QLEN, DLEN + 1), jax.random.fold_in(streams_of[4], 1), QLEN, DLEN).astype(jnp.int32),
        "matching_pair": jax.vmap(lambda own: jax.random.permutation(own, PAIRS_ALL))(jax.random.split(streams_of[5], MICRO)).reshape((MICRO, PAIRS_ALL)).astype(jnp.int32),
        "steepness_pair": draw_steepness_pair(jax.random.fold_in(streams_of[7], 71), 0),
    }


EPSILON = 1e-06
OBJECTIVE_FACTOR = 1024.0
MASKED = -1e+30

def head_forward(token_rows, rescale_factor, embedding_matrix):
    values = token_rows.astype(jnp.float32)
    inverse_rms = lax.rsqrt(lax.optimization_barrier(jnp.mean(values * values, axis=-1, keepdims=True)) + EPSILON)
    normed = (values * inverse_rms * rescale_factor).astype(jnp.bfloat16)
    projected = jnp.dot(normed, embedding_matrix, preferred_element_type=jnp.float32)
    inverse_length = lax.rsqrt(lax.optimization_barrier(jnp.sum(projected * projected, axis=-1, keepdims=True)) + EPSILON)
    vectors = (projected * inverse_length).astype(jnp.bfloat16)
    return (vectors, projected, inverse_length, inverse_rms)

def head_backward(token_rows, rescale_factor, embedding_matrix, projected, inverse_length, inverse_rms, grad_vectors):
    unit = projected * inverse_length
    along = lax.optimization_barrier(jnp.sum(unit * grad_vectors, axis=-1, keepdims=True))
    grad_projected = (inverse_length * (grad_vectors - unit * along)).astype(jnp.bfloat16)
    grad_normed = lax.dot_general(grad_projected, embedding_matrix, (((1,), (1,)), ((), ())), preferred_element_type=jnp.float32)
    values = token_rows.astype(jnp.float32)
    weighted = grad_normed * rescale_factor
    mean_term = lax.optimization_barrier(jnp.mean(values * weighted, axis=-1, keepdims=True))
    grad_rows = inverse_rms * weighted - values * (inverse_rms * inverse_rms * inverse_rms) * mean_term
    return grad_rows.astype(jnp.bfloat16)

def pool_tokens(similarity, pooling_steepness, live):
    scaled = jnp.where(live[None], pooling_steepness * similarity, MASKED)
    highest = lax.optimization_barrier(jnp.max(scaled, axis=2, keepdims=True))
    exponent = jnp.exp(scaled - highest)
    totals = lax.optimization_barrier(jnp.sum(exponent, axis=2, keepdims=True))
    smooth = (highest[:, :, 0] + jnp.log(totals[:, :, 0])) / pooling_steepness
    return (smooth, exponent / totals)

def versus_term(relevance_matrix, matching_pair, logit_multiplier):
    unnormalized_odds = logit_multiplier * relevance_matrix
    highest = lax.optimization_barrier(jnp.max(unnormalized_odds, axis=1, keepdims=True))
    log_total = highest[:, 0] + jnp.log(lax.optimization_barrier(jnp.sum(jnp.exp(unnormalized_odds - highest), axis=1)))
    columns = jnp.arange(relevance_matrix.shape[1], dtype=jnp.int32)
    correct_label = (columns[None, :] == matching_pair[:, None]).astype(jnp.float32)
    objective_value = log_total - lax.optimization_barrier(jnp.sum(unnormalized_odds * correct_label, axis=1))
    probability_share = jnp.exp(unnormalized_odds - log_total[:, None])
    score_slope = OBJECTIVE_FACTOR * logit_multiplier * (probability_share - correct_label)
    return (objective_value, score_slope)

def query_weights(request_span, count):
    places = jnp.arange(count, dtype=jnp.int32)
    ones = jnp.where(places[None, :] < request_span[:, None], 1.0, 0.0).astype(jnp.float32)
    return ones / request_span[:, None].astype(jnp.float32)

def live_tokens(passage_span, count):
    places = jnp.arange(count, dtype=jnp.int32)
    return places[None, :] < passage_span[:, None]

def single_micro_group(piece_tile, request_spans, passage_spans, selected_entry, rescale_factor, embedding_matrix, pooling_steepness, logit_multiplier):
    pairs, length, width = piece_tile.shape
    flat_rows = piece_tile.reshape(pairs * length, width)
    vectors, projected, inverse_length, inverse_rms = head_forward(flat_rows, rescale_factor, embedding_matrix)
    vectors = vectors.reshape(pairs, length, -1)
    features = vectors.shape[2]
    queries = vectors[:, :QLEN]
    doc_flat = vectors[:, QLEN:].reshape(pairs * DLEN, features)
    live = live_tokens(passage_spans, DLEN)
    weights = query_weights(request_spans, QLEN)

    def similarity_of(index):
        query = lax.dynamic_index_in_dim(queries, index, 0, keepdims=False)
        inner_product = lax.dot_general(query, doc_flat, (((1,), (1,)), ((), ())), preferred_element_type=jnp.float32)
        return (inner_product.reshape(QLEN, pairs, DLEN), query)

    def forward_pass(index):
        similarity, _ = similarity_of(index)
        smooth, _ = pool_tokens(similarity, pooling_steepness, live)
        row_weight = lax.dynamic_index_in_dim(weights, index, 0, keepdims=False)
        return lax.optimization_barrier(jnp.sum(smooth * row_weight[:, None], axis=0))
    indices = jnp.arange(pairs, dtype=jnp.int32)
    relevance_matrix = lax.map(forward_pass, indices)
    objective_value, score_slope = versus_term(relevance_matrix, selected_entry, logit_multiplier)

    def backward(carry, index):
        similarity, query = similarity_of(index)
        _, token_weight = pool_tokens(similarity, pooling_steepness, live)
        row_weight = lax.dynamic_index_in_dim(weights, index, 0, keepdims=False)
        grad_row = lax.dynamic_index_in_dim(score_slope, index, 0, keepdims=False)
        coefficient = row_weight[:, None] * grad_row[None, :]
        similarity_gradient = (coefficient[:, :, None] * token_weight).astype(jnp.bfloat16).reshape(QLEN, pairs * DLEN)
        grad_query = jnp.dot(similarity_gradient, doc_flat, preferred_element_type=jnp.float32)
        carry = carry + lax.dot_general(similarity_gradient, query, (((0,), (0,)), ((), ())), preferred_element_type=jnp.float32)
        return (carry, grad_query)
    grad_docs, grad_queries = lax.scan(backward, jnp.zeros((pairs * DLEN, features), jnp.float32), indices)
    grad_vectors = jnp.concatenate([grad_queries.reshape(pairs, QLEN, features), grad_docs.reshape(pairs, DLEN, features)], axis=1)
    grad_rows = head_backward(flat_rows, rescale_factor, embedding_matrix, projected, inverse_length, inverse_rms, grad_vectors.reshape(pairs * length, features))
    return (grad_rows.reshape(pairs, length, width), objective_value)

def reference(latent_states, rescale_factor, embedding_matrix, request_span, passage_span, matching_pair, steepness_pair):
    pooling_steepness = steepness_pair[0]
    logit_multiplier = steepness_pair[1]

    def per_batch(inputs):
        piece_tile, request_spans, passage_spans, selected_entry = inputs
        return single_micro_group(piece_tile, request_spans, passage_spans, selected_entry, rescale_factor, embedding_matrix, pooling_steepness, logit_multiplier)
    grad_hidden, losses = lax.map(per_batch, (latent_states, request_span, passage_span, matching_pair))
    return (grad_hidden, losses)
```

```python
import functools

import jax
import jax.numpy as jnp
from jax import lax
from jax.experimental import pallas as pl
from jax.experimental.pallas import tpu as pltpu
from jax.sharding import PartitionSpec as P

QLEN = 32
DLEN = 64

EPSILON = 1e-06
OBJECTIVE_FACTOR = 1024.0
MASKED = -1e30

ROWS = 16
CHUNKS = 2


def dot(a, b, dims, precision=None):
    return lax.dot_general(
        a, b, (dims, ((), ())), precision=precision, preferred_element_type=jnp.float32
    )


def body(
    n,
    sections,
    x_hbm,
    gain_ref,
    w_hbm,
    request_ref,
    passage_ref,
    match_ref,
    steep_ref,
    out_hbm,
    loss_ref,
    xbuf,
    nrm,
    wbuf,
    proj,
    qinv,
    rinv,
    docs,
    queries,
    e_own,
    e_all,
    gbuf,
    gqbuf,
    gnbuf,
    obuf,
    smooth_own,
    tinv_own,
    smooth_all,
    tinv_all,
    label_own,
    label_all,
    weight_all,
    lse_buf,
    x_sem,
    w_sem,
    wsend,
    wrecv,
    dsend,
    drecv,
    qsend,
    qrecv,
    lsend,
    lrecv,
    osem,
):
    pairs, length, width = xbuf.shape
    depth = wbuf.shape[1]
    lanes = pairs * QLEN
    section = lax.axis_index("section")
    me = lax.axis_index("dp")

    half = n // 2
    col = me % 2
    pos = (me // 2) * (1 - col) + (n - 1 - me // 2) * col

    def device_at(p):
        side = p // half
        return 2 * (p * (1 - side) + (n - 1 - p) * side) + side

    def owner_of(slot):
        return device_at((pos + n - slot) % n)

    right = device_at((pos + 1) % n)
    left = device_at((pos + n - 1) % n)

    chips = sections // 2
    core = section % 2
    chip = section // 2
    partner = chip * 2 + 1 - core

    def over(t):
        return ((chip + t) % chips) * 2 + core

    def remote(src, dst, send, recv, axis, index):
        return pltpu.make_async_remote_copy(
            src_ref=src,
            dst_ref=dst,
            send_sem=send,
            recv_sem=recv,
            device_id={axis: index},
            device_id_type=pl.DeviceIdType.MESH,
        )

    x_copies = [
        pltpu.make_async_copy(x_hbm.at[0, b], xbuf.at[b], x_sem.at[b]) for b in range(pairs)
    ]
    w_copy = pltpu.make_async_copy(w_hbm, wbuf.at[section], w_sem)
    w_copy.start()
    for copy in x_copies:
        copy.start()

    barrier = pltpu.get_barrier_semaphore()
    greeted = [("section", partner)]
    greeted += [("section", over(t)) for t in range(1, chips)]
    greeted += [("dp", right), ("dp", left)]
    for axis, index in greeted:
        pl.semaphore_signal(
            barrier, inc=1, device_id={axis: index}, device_id_type=pl.DeviceIdType.MESH
        )
    pl.semaphore_wait(barrier, len(greeted))

    part = depth // CHUNKS
    started = []

    def launch(copy):
        copy.start()
        started.append(copy)

    def piece(ref, index, h):
        return ref.at[index, pl.ds(h * part, part)]

    for t in range(1, chips):
        for h in range(CHUNKS):
            launch(
                remote(
                    w_hbm.at[pl.ds(h * part, part)],
                    piece(wbuf, section, h),
                    wsend.at[t, h],
                    wrecv.at[t, h],
                    "section",
                    over(t),
                )
            )
    for h in range(CHUNKS):
        launch(
            remote(
                w_hbm.at[pl.ds(h * part, part)],
                piece(wbuf, section, h),
                wsend.at[0, h],
                wrecv.at[0, h],
                "section",
                partner,
            )
        )

    gain = gain_ref[...]
    for b in range(pairs):
        x_copies[b].wait()

        def norm_rows(i, carry, b=b):
            r = pl.multiple_of(i * ROWS, ROWS)
            v = xbuf[b, pl.ds(r, ROWS), :].astype(jnp.float32)
            q = lax.rsqrt(jnp.sum(v * v, axis=1, keepdims=True) * (1.0 / width) + EPSILON)
            full = pl.multiple_of(b * length + i * ROWS, ROWS)
            qinv[pl.ds(full, ROWS), :] = jnp.broadcast_to(q, (ROWS, 128))
            z = (v * q * gain).astype(jnp.bfloat16)
            for k in range(sections):
                nrm[k, pl.ds(full, ROWS), :] = z[:, k * depth : (k + 1) * depth]
            return carry

        lax.fori_loop(0, length // ROWS, norm_rows, 0, unroll=2)

    def add_piece(index, first=False):
        term = dot(nrm[index], wbuf[index], ((1,), (0,)))
        proj[...] = term if first else proj[...] + term

    w_copy.wait()
    add_piece(section, True)
    for h in range(CHUNKS):
        place = piece(wbuf, partner, h)
        remote(place, place, wsend.at[0, h], wrecv.at[0, h], "section", partner).wait_recv()
    add_piece(partner)
    for t in range(1, chips):
        source = over(chips - t)
        for h in range(CHUNKS):
            place = piece(wbuf, source, h)
            remote(place, place, wsend.at[t, h], wrecv.at[t, h], "section", partner).wait_recv()
            launch(
                remote(
                    place,
                    place,
                    wsend.at[chips + t, h],
                    wrecv.at[chips + t, h],
                    "section",
                    partner,
                )
            )
        add_piece(source)
    for t in range(1, chips):
        source = ((chip + chips - t) % chips) * 2 + 1 - core
        for h in range(CHUNKS):
            place = piece(wbuf, source, h)
            remote(
                place, place, wsend.at[chips + t, h], wrecv.at[chips + t, h], "section", partner
            ).wait_recv()
        add_piece(source)

    for b in range(pairs):
        p = proj[b * length : (b + 1) * length, :]
        r = lax.rsqrt(jnp.sum(p * p, axis=1, keepdims=True) + EPSILON)
        rinv[b * length : (b + 1) * length, :] = jnp.broadcast_to(r, p.shape)
        v = (p * r).astype(jnp.bfloat16)
        queries[0, b * QLEN : (b + 1) * QLEN, :] = v[:QLEN]
        docs[0, b * DLEN : (b + 1) * DLEN, :] = v[QLEN:]

    def onward(buf, send, recv, slot, ascending):
        to = slot + 1 if ascending else (n if slot == 0 else slot) - 1
        return remote(
            buf.at[slot],
            buf.at[to],
            send.at[0 if ascending else 1, slot],
            recv.at[to],
            "dp",
            right if ascending else left,
        )

    chains = [
        (docs, dsend, drecv, True, n // 2),
        (docs, dsend, drecv, False, n - 1 - n // 2),
        (queries, qsend, qrecv, True, n - 1 - n // 2),
        (queries, qsend, qrecv, False, n // 2),
    ]
    for buf, send, recv, ascending, reach in chains:
        if reach > 0:
            launch(onward(buf, send, recv, 0, ascending))

    beta = steep_ref[0]
    sharp = steep_ref[1]
    inverse_beta = 1.0 / jnp.full((1, lanes), beta, jnp.float32)
    place_j = lax.broadcasted_iota(jnp.int32, (DLEN, lanes), 0)
    lane = lax.broadcasted_iota(jnp.int32, (1, lanes), 1)
    lane_pair = lane // QLEN
    lane_token = lane % QLEN

    def spread(ref, first):
        value = jnp.full((1, lanes), ref[section, first], jnp.int32)
        for b in range(1, pairs):
            value = jnp.where(lane_pair == b, ref[section, first + b], value)
        return value

    def weights_of(owner):
        span = spread(request_ref, owner * pairs)
        return jnp.where(lane_token < span, 1.0 / span.astype(jnp.float32), 0.0)

    def forward(doc_rows, query_rows, owner, slot, e_ref, smooth_ref, tinv_ref):
        s = dot(doc_rows, query_rows, ((1,), (1,)))
        for c in range(pairs):
            span = passage_ref[section, owner * pairs + c]
            sc = jnp.where(place_j < span, beta * s[c * DLEN : (c + 1) * DLEN], MASKED)
            high = jnp.max(sc, axis=0, keepdims=True)
            e = jnp.exp(sc - high)
            total = jnp.sum(e, axis=0, keepdims=True)
            e_ref[slot, c * DLEN : (c + 1) * DLEN, :] = e
            row = slot * pairs + c
            smooth_ref[row : row + 1, :] = (high + jnp.log(total)) * inverse_beta
            tinv_ref[row : row + 1, :] = 1.0 / total

    own_weight = weights_of(me)
    own_match = spread(match_ref, me * pairs)

    def own_forward(slot):
        owner = owner_of(slot)
        forward(docs[slot], queries[0], owner, slot, e_own, smooth_own, tinv_own)
        for c in range(pairs):
            row = slot * pairs + c
            label_own[row : row + 1, :] = jnp.where(own_match == owner * pairs + c, 1.0, 0.0)

    own_forward(0)
    for slot in range(n):
        owner = owner_of(slot)
        match = spread(match_ref, owner * pairs)
        weight = weights_of(owner)
        for c in range(pairs):
            row = slot * pairs + c
            label_all[row : row + 1, :] = jnp.where(match == me * pairs + c, 1.0, 0.0)
            weight_all[row : row + 1, :] = weight
    for d in range(1, n // 2 + 1):
        for buf, send, recv, ascending, reach in chains:
            if reach >= d:
                slot = d if ascending else n - d
                place = buf.at[slot]
                remote(place, place, send.at[0, 0], recv.at[slot], "dp", right).wait_recv()
                if reach > d:
                    launch(onward(buf, send, recv, slot, ascending))
        for slot in sorted({d, n - d}):
            own_forward(slot)

    from_lane = lax.broadcasted_iota(jnp.int32, (lanes, lanes), 0) // QLEN
    to_lane = lax.broadcasted_iota(jnp.int32, (lanes, lanes), 1) // QLEN
    same = jnp.where(from_lane == to_lane, 1.0, 0.0)
    highest = lax.Precision.HIGHEST
    scores = dot(smooth_own[...] * own_weight, same, ((1,), (0,)), highest)
    logits = sharp * scores
    high = jnp.max(logits, axis=0, keepdims=True)
    lse = high + jnp.log(jnp.sum(jnp.exp(logits - high), axis=0, keepdims=True))
    lse_buf[0] = jnp.broadcast_to(lse, (8, lanes))
    for k in range(1, n):
        launch(
            remote(
                lse_buf.at[0],
                lse_buf.at[k],
                lsend.at[k],
                lrecv.at[k],
                "dp",
                device_at((pos + k) % n),
            )
        )
    label = label_own[...]
    loss = lse - jnp.sum(logits * label, axis=0, keepdims=True)
    for b in range(pairs):
        loss_ref[:, b : b + 1] = loss[:, b * QLEN : b * QLEN + 1]
    slope = OBJECTIVE_FACTOR * sharp * (jnp.exp(logits - lse) - label)
    tinv_own[...] = own_weight * slope * tinv_own[...]

    def grads(slot, e_ref, coefficient_ref):
        for c in range(pairs):
            row = slot * pairs + c
            gbuf[slot, c * DLEN : (c + 1) * DLEN, :] = (
                coefficient_ref[row : row + 1, :] * e_ref[slot, c * DLEN : (c + 1) * DLEN, :]
            ).astype(jnp.bfloat16)

    for slot in range(n):
        grads(slot, e_own, tinv_own)
    grad_query = dot(
        gbuf[...].reshape(n * pairs * DLEN, lanes),
        docs[...].reshape(n * pairs * DLEN, docs.shape[2]),
        ((0,), (0,)),
    )

    all_w = wbuf[...].reshape(sections * depth, wbuf.shape[2])
    out_copies = []

    def head_backward(gradient, first, count):
        for b in range(pairs):
            lo = b * length + first
            g = gradient[b * count : (b + 1) * count]
            r = rinv[lo : lo + count, :]
            u = proj[lo : lo + count, :] * r
            along = jnp.sum(u * g, axis=1, keepdims=True)
            gqbuf[b * count : (b + 1) * count, :] = (r * (g - u * along)).astype(jnp.bfloat16)
        gnbuf[0 : pairs * count, :] = dot(gqbuf[0 : pairs * count, :], all_w, ((1,), (1,)))
        for b in range(pairs):

            def rows(i, carry, b=b):
                r = pl.multiple_of(first + i * ROWS, ROWS)
                v = xbuf[b, pl.ds(r, ROWS), :].astype(jnp.float32)
                at = pl.multiple_of(b * count + i * ROWS, ROWS)
                weighted = gnbuf[pl.ds(at, ROWS), :] * gain
                mean = jnp.sum(v * weighted, axis=1, keepdims=True) * (1.0 / width)
                full = pl.multiple_of(b * length + first + i * ROWS, ROWS)
                q = qinv[pl.ds(full, ROWS), :][:, 0:1]
                obuf[b, pl.ds(r, ROWS), :] = (q * weighted - v * (q * q * q * mean)).astype(
                    jnp.bfloat16
                )
                return carry

            lax.fori_loop(0, count // ROWS, rows, 0, unroll=2)
            copy = pltpu.make_async_copy(
                obuf.at[b, pl.ds(first, count)],
                out_hbm.at[0, b, pl.ds(first, count)],
                osem.at[0 if first == 0 else 1, b],
            )
            copy.start()
            out_copies.append(copy)

    head_backward(grad_query, 0, QLEN)

    for slot in range(n):
        forward(docs[0], queries[slot], me, slot, e_all, smooth_all, tinv_all)
    weight = weight_all[...]
    logits = sharp * dot(smooth_all[...] * weight, same, ((1,), (0,)), highest)
    smooth_all[...] = logits
    for slot in range(n):
        rows = slice(slot * pairs, (slot + 1) * pairs)
        if slot:
            place = lse_buf.at[slot]
            remote(place, place, lsend.at[slot], lrecv.at[slot], "dp", right).wait_recv()
        share = jnp.exp(smooth_all[rows, :] - lse_buf[slot][0:1])
        slope = OBJECTIVE_FACTOR * sharp * (share - label_all[rows, :])
        tinv_all[rows, :] = weight_all[rows, :] * slope * tinv_all[rows, :]
    grad_doc = jnp.zeros((pairs * DLEN, docs.shape[2]), jnp.float32)
    for slot in range(n):
        grads(slot, e_all, tinv_all)
        grad_doc = grad_doc + dot(gbuf[slot], queries[slot], ((1,), (0,)))
    head_backward(grad_doc, QLEN, DLEN)

    for copy in started:
        copy.wait_send()
    for copy in out_copies:
        copy.wait()


def local(
    n,
    sections,
    latent_states,
    rescale_factor,
    embedding_matrix,
    request_span,
    passage_span,
    matching_pair,
    steepness_pair,
):
    _, pairs, length, width = latent_states.shape
    depth, features = embedding_matrix.shape
    rows = pairs * length
    lanes = pairs * QLEN
    f32, bf16 = jnp.float32, jnp.bfloat16
    dma = pltpu.SemaphoreType.DMA
    vmem = pl.BlockSpec(memory_space=pltpu.VMEM)
    smem = pl.BlockSpec(memory_space=pltpu.SMEM)
    anywhere = pl.BlockSpec(memory_space=pl.ANY)
    chips = sections // 2
    return pl.pallas_call(
        functools.partial(body, n, sections),
        out_shape=(
            jax.ShapeDtypeStruct(latent_states.shape, bf16),
            jax.ShapeDtypeStruct((1, pairs), f32),
        ),
        in_specs=[anywhere, vmem, anywhere, smem, smem, smem, smem],
        out_specs=(anywhere, vmem),
        scratch_shapes=[
            pltpu.VMEM((pairs, length, width), bf16),
            pltpu.VMEM((sections, rows, depth), bf16),
            pltpu.VMEM((sections, depth, features), bf16),
            pltpu.VMEM((rows, features), f32),
            pltpu.VMEM((rows, 128), f32),
            pltpu.VMEM((rows, features), f32),
            pltpu.VMEM((n, pairs * DLEN, features), bf16),
            pltpu.VMEM((n, pairs * QLEN, features), bf16),
            pltpu.VMEM((n, pairs * DLEN, lanes), f32),
            pltpu.VMEM((n, pairs * DLEN, lanes), f32),
            pltpu.VMEM((n, pairs * DLEN, lanes), bf16),
            pltpu.VMEM((pairs * DLEN, features), bf16),
            pltpu.VMEM((pairs * DLEN, width), f32),
            pltpu.VMEM((pairs, length, width), bf16),
            pltpu.VMEM((n * pairs, lanes), f32),
            pltpu.VMEM((n * pairs, lanes), f32),
            pltpu.VMEM((n * pairs, lanes), f32),
            pltpu.VMEM((n * pairs, lanes), f32),
            pltpu.VMEM((n * pairs, lanes), f32),
            pltpu.VMEM((n * pairs, lanes), f32),
            pltpu.VMEM((n * pairs, lanes), f32),
            pltpu.VMEM((n, 8, lanes), f32),
            dma((pairs,)),
            dma(()),
            dma((2 * chips, CHUNKS)),
            dma((2 * chips, CHUNKS)),
            dma((2, n)),
            dma((n,)),
            dma((2, n)),
            dma((n,)),
            dma((n,)),
            dma((n,)),
            dma((2, pairs)),
        ],
        compiler_params=pltpu.CompilerParams(
            collective_id=0, has_side_effects=True, vmem_limit_bytes=60 * 1024 * 1024
        ),
        name="late_interaction",
    )(
        latent_states,
        rescale_factor.reshape(1, width),
        embedding_matrix,
        request_span,
        passage_span,
        matching_pair,
        steepness_pair,
    )


def solution(mesh):
    return jax.shard_map(
        functools.partial(local, mesh.shape["dp"], mesh.shape["section"]),
        mesh=mesh,
        in_specs=(P("section", "dp", None, None), P(), P("section", None), P(), P(), P(), P()),
        out_specs=(P("section", "dp", None, None), P("section", "dp")),
        check_vma=False,
    )
```

```python
import functools

import jax
import jax.numpy as jnp
from jax import lax
from jax.experimental import pallas as pl
from jax.experimental.pallas import tpu as pltpu
from jax.sharding import PartitionSpec as P

QLEN = 32
DLEN = 64

EPSILON = 1e-06
OBJECTIVE_FACTOR = 1024.0
MASKED = -1e30

ROWS = 16
CHUNKS = 4
QUERY_CHUNKS = 2
DOC_CHUNKS = 4


def dot(a, b, dims, precision=None):
    return lax.dot_general(
        a, b, (dims, ((), ())), precision=precision, preferred_element_type=jnp.float32
    )


def body(
    n,
    sections,
    x_hbm,
    gain_ref,
    w_hbm,
    request_ref,
    passage_ref,
    match_ref,
    steep_ref,
    out_hbm,
    loss_ref,
    xbuf,
    nrm,
    wbuf,
    proj,
    qinv,
    rinv,
    docs,
    queries,
    e_own,
    e_all,
    gbuf,
    gqbuf,
    gnbuf,
    obuf,
    smooth_own,
    tinv_own,
    smooth_all,
    tinv_all,
    label_own,
    label_all,
    weight_all,
    lse_buf,
    x_sem,
    w_sem,
    wsend,
    wrecv,
    dsend,
    drecv,
    qsend,
    qrecv,
    lsend,
    lrecv,
    osem,
):
    pairs, length, width = xbuf.shape
    depth = wbuf.shape[1]
    lanes = pairs * QLEN
    section = lax.axis_index("section")
    me = lax.axis_index("dp")

    half = n // 2
    col = me % 2
    pos = (me // 2) * (1 - col) + (n - 1 - me // 2) * col

    def device_at(p):
        side = p // half
        return 2 * (p * (1 - side) + (n - 1 - p) * side) + side

    def owner_of(slot):
        return device_at((pos + n - slot) % n)

    right = device_at((pos + 1) % n)
    left = device_at((pos + n - 1) % n)

    chips = sections // 2
    core = section % 2
    chip = section // 2
    partner = chip * 2 + 1 - core

    def over(t):
        return ((chip + t) % chips) * 2 + core

    def remote(src, dst, send, recv, axis, index):
        return pltpu.make_async_remote_copy(
            src_ref=src,
            dst_ref=dst,
            send_sem=send,
            recv_sem=recv,
            device_id={axis: index},
            device_id_type=pl.DeviceIdType.MESH,
        )

    x_copies = [
        pltpu.make_async_copy(x_hbm.at[0, b], xbuf.at[b], x_sem.at[b]) for b in range(pairs)
    ]
    w_copy = pltpu.make_async_copy(w_hbm, wbuf.at[section], w_sem)
    w_copy.start()
    for copy in x_copies:
        copy.start()

    barrier = pltpu.get_barrier_semaphore()
    greeted = [("section", partner)]
    greeted += [("section", over(t)) for t in range(1, chips)]
    greeted += [("dp", right), ("dp", left)]
    for axis, index in greeted:
        pl.semaphore_signal(
            barrier, inc=1, device_id={axis: index}, device_id_type=pl.DeviceIdType.MESH
        )
    pl.semaphore_wait(barrier, len(greeted))

    part = depth // CHUNKS
    started = []

    def launch(copy):
        copy.start()
        started.append(copy)

    def piece(ref, index, h):
        return ref.at[index, pl.ds(h * part, part)]

    for t in range(1, chips):
        for h in range(CHUNKS):
            launch(
                remote(
                    w_hbm.at[pl.ds(h * part, part)],
                    piece(wbuf, section, h),
                    wsend.at[t, h],
                    wrecv.at[t, h],
                    "section",
                    over(t),
                )
            )
    for h in range(CHUNKS):
        launch(
            remote(
                w_hbm.at[pl.ds(h * part, part)],
                piece(wbuf, section, h),
                wsend.at[0, h],
                wrecv.at[0, h],
                "section",
                partner,
            )
        )

    gain = gain_ref[...]
    for b in range(pairs):
        x_copies[b].wait()

        def norm_rows(i, carry, b=b):
            r = pl.multiple_of(i * ROWS, ROWS)
            v = xbuf[b, pl.ds(r, ROWS), :].astype(jnp.float32)
            q = lax.rsqrt(jnp.sum(v * v, axis=1, keepdims=True) * (1.0 / width) + EPSILON)
            full = pl.multiple_of(b * length + i * ROWS, ROWS)
            qinv[pl.ds(full, ROWS), :] = jnp.broadcast_to(q, (ROWS, 128))
            z = (v * q * gain).astype(jnp.bfloat16)
            for k in range(sections):
                nrm[k, pl.ds(full, ROWS), :] = z[:, k * depth : (k + 1) * depth]
            return carry

        lax.fori_loop(0, length // ROWS, norm_rows, 0, unroll=2)

    def add_piece(index, first=False):
        term = dot(nrm[index], wbuf[index], ((1,), (0,)))
        proj[...] = term if first else proj[...] + term

    w_copy.wait()
    add_piece(section, True)
    for h in range(CHUNKS):
        place = piece(wbuf, partner, h)
        remote(place, place, wsend.at[0, h], wrecv.at[0, h], "section", partner).wait_recv()
    add_piece(partner)
    for t in range(1, chips):
        source = over(chips - t)
        for h in range(CHUNKS):
            place = piece(wbuf, source, h)
            remote(place, place, wsend.at[t, h], wrecv.at[t, h], "section", partner).wait_recv()
            launch(
                remote(
                    place,
                    place,
                    wsend.at[chips + t, h],
                    wrecv.at[chips + t, h],
                    "section",
                    partner,
                )
            )
        add_piece(source)
    for t in range(1, chips):
        source = ((chip + chips - t) % chips) * 2 + 1 - core
        for h in range(CHUNKS):
            place = piece(wbuf, source, h)
            remote(
                place, place, wsend.at[chips + t, h], wrecv.at[chips + t, h], "section", partner
            ).wait_recv()
        add_piece(source)

    for b in range(pairs):
        p = proj[b * length : (b + 1) * length, :]
        r = lax.rsqrt(jnp.sum(p * p, axis=1, keepdims=True) + EPSILON)
        rinv[b * length : (b + 1) * length, :] = jnp.broadcast_to(r, p.shape)
        v = (p * r).astype(jnp.bfloat16)
        queries[0, b * QLEN : (b + 1) * QLEN, :] = v[:QLEN]
        docs[0, b * DLEN : (b + 1) * DLEN, :] = v[QLEN:]

    def chunk(buf, slot, h, count):
        size = buf.shape[1] // count
        return buf.at[slot, pl.ds(h * size, size)]

    def onward(chain, slot, h):
        buf, send, recv, ascending, _, count = chain
        to = slot + 1 if ascending else (n if slot == 0 else slot) - 1
        return remote(
            chunk(buf, slot, h, count),
            chunk(buf, to, h, count),
            send.at[0 if ascending else 1, slot, h],
            recv.at[to, h],
            "dp",
            right if ascending else left,
        )

    query_chains = [
        (queries, qsend, qrecv, True, n // 2, QUERY_CHUNKS),
        (queries, qsend, qrecv, False, n - 1 - n // 2, QUERY_CHUNKS),
    ]
    doc_chains = [
        (docs, dsend, drecv, True, n - 1 - n // 2, DOC_CHUNKS),
        (docs, dsend, drecv, False, n // 2, DOC_CHUNKS),
    ]

    def pass_on(chains, d):
        for h in range(chains[0][5]):
            for chain in chains:
                buf, send, recv, ascending, reach, count = chain
                if d > 0 and reach >= d:
                    slot = d if ascending else n - d
                    place = chunk(buf, slot, h, count)
                    remote(
                        place, place, send.at[0, 0, h], recv.at[slot, h], "dp", right
                    ).wait_recv()
                if reach > d:
                    launch(onward(chain, d if ascending else (n - d) % n, h))

    pass_on(query_chains, 0)
    pass_on(doc_chains, 0)

    beta = steep_ref[0]
    sharp = steep_ref[1]
    inverse_beta = 1.0 / jnp.full((1, lanes), beta, jnp.float32)
    place_j = lax.broadcasted_iota(jnp.int32, (DLEN, lanes), 0)
    lane = lax.broadcasted_iota(jnp.int32, (1, lanes), 1)
    lane_pair = lane // QLEN
    lane_token = lane % QLEN

    def spread(ref, first):
        value = jnp.full((1, lanes), ref[section, first], jnp.int32)
        for b in range(1, pairs):
            value = jnp.where(lane_pair == b, ref[section, first + b], value)
        return value

    def weights_of(owner):
        span = spread(request_ref, owner * pairs)
        return jnp.where(lane_token < span, 1.0 / span.astype(jnp.float32), 0.0)

    def forward(doc_rows, query_rows, owner, slot, e_ref, smooth_ref, tinv_ref):
        s = dot(doc_rows, query_rows, ((1,), (1,)))
        for c in range(pairs):
            span = passage_ref[section, owner * pairs + c]
            sc = jnp.where(place_j < span, beta * s[c * DLEN : (c + 1) * DLEN], MASKED)
            high = jnp.max(sc, axis=0, keepdims=True)
            e = jnp.exp(sc - high)
            total = jnp.sum(e, axis=0, keepdims=True)
            e_ref[slot, c * DLEN : (c + 1) * DLEN, :] = e
            row = slot * pairs + c
            smooth_ref[row : row + 1, :] = (high + jnp.log(total)) * inverse_beta
            tinv_ref[row : row + 1, :] = 1.0 / total

    own_weight = weights_of(me)
    own_match = spread(match_ref, me * pairs)

    def own_forward(slot):
        owner = owner_of(slot)
        forward(docs[slot], queries[0], owner, slot, e_own, smooth_own, tinv_own)
        for c in range(pairs):
            row = slot * pairs + c
            label_own[row : row + 1, :] = jnp.where(own_match == owner * pairs + c, 1.0, 0.0)

    def doc_forward(slot):
        forward(docs[0], queries[slot], me, slot, e_all, smooth_all, tinv_all)

    doc_forward(0)
    own_forward(0)
    for slot in range(n):
        owner = owner_of(slot)
        match = spread(match_ref, owner * pairs)
        weight = weights_of(owner)
        for c in range(pairs):
            row = slot * pairs + c
            label_all[row : row + 1, :] = jnp.where(match == me * pairs + c, 1.0, 0.0)
            weight_all[row : row + 1, :] = weight

    from_lane = lax.broadcasted_iota(jnp.int32, (lanes, lanes), 0) // QLEN
    to_lane = lax.broadcasted_iota(jnp.int32, (lanes, lanes), 1) // QLEN
    same = jnp.where(from_lane == to_lane, 1.0, 0.0)
    highest = lax.Precision.HIGHEST

    for d in range(1, n // 2 + 1):
        pass_on(query_chains, d)
        for slot in sorted({d, n - d}):
            doc_forward(slot)
        if d == n // 2:
            smooth_all[...] = sharp * dot(
                smooth_all[...] * weight_all[...], same, ((1,), (0,)), highest
            )
            for slot in range(n):
                logits = smooth_all[slot * pairs : (slot + 1) * pairs, :]
                high = jnp.max(logits, axis=0, keepdims=True)
                lse_buf[0, slot : slot + 1, :] = high + jnp.log(
                    jnp.sum(jnp.exp(logits - high), axis=0, keepdims=True)
                )
            for k in range(1, n):
                launch(
                    remote(
                        lse_buf.at[0],
                        lse_buf.at[k],
                        lsend.at[k],
                        lrecv.at[k],
                        "dp",
                        device_at((pos + k) % n),
                    )
                )
        pass_on(doc_chains, d)
        for slot in sorted({d, n - d}):
            own_forward(slot)

    scores = dot(smooth_own[...] * own_weight, same, ((1,), (0,)), highest)
    logits = sharp * scores
    high = jnp.max(logits, axis=0, keepdims=True)
    lse = high + jnp.log(jnp.sum(jnp.exp(logits - high), axis=0, keepdims=True))
    label = label_own[...]
    loss = lse - jnp.sum(logits * label, axis=0, keepdims=True)
    for b in range(pairs):
        loss_ref[:, b : b + 1] = loss[:, b * QLEN : b * QLEN + 1]
    slope = OBJECTIVE_FACTOR * sharp * (jnp.exp(logits - lse) - label)
    tinv_own[...] = own_weight * slope * tinv_own[...]

    def grads(slot, e_ref, coefficient_ref):
        for c in range(pairs):
            row = slot * pairs + c
            gbuf[slot, c * DLEN : (c + 1) * DLEN, :] = (
                coefficient_ref[row : row + 1, :] * e_ref[slot, c * DLEN : (c + 1) * DLEN, :]
            ).astype(jnp.bfloat16)

    for slot in range(n):
        grads(slot, e_own, tinv_own)
    grad_query = dot(
        gbuf[...].reshape(n * pairs * DLEN, lanes),
        docs[...].reshape(n * pairs * DLEN, docs.shape[2]),
        ((0,), (0,)),
    )

    all_w = wbuf[...].reshape(sections * depth, wbuf.shape[2])
    out_copies = []

    def head_backward(gradient, first, count):
        for b in range(pairs):
            lo = b * length + first
            g = gradient[b * count : (b + 1) * count]
            r = rinv[lo : lo + count, :]
            u = proj[lo : lo + count, :] * r
            along = jnp.sum(u * g, axis=1, keepdims=True)
            gqbuf[b * count : (b + 1) * count, :] = (r * (g - u * along)).astype(jnp.bfloat16)
        gnbuf[0 : pairs * count, :] = dot(gqbuf[0 : pairs * count, :], all_w, ((1,), (1,)))
        for b in range(pairs):

            def rows(i, carry, b=b):
                r = pl.multiple_of(first + i * ROWS, ROWS)
                v = xbuf[b, pl.ds(r, ROWS), :].astype(jnp.float32)
                at = pl.multiple_of(b * count + i * ROWS, ROWS)
                weighted = gnbuf[pl.ds(at, ROWS), :] * gain
                mean = jnp.sum(v * weighted, axis=1, keepdims=True) * (1.0 / width)
                full = pl.multiple_of(b * length + first + i * ROWS, ROWS)
                q = qinv[pl.ds(full, ROWS), :][:, 0:1]
                obuf[b, pl.ds(r, ROWS), :] = (q * weighted - v * (q * q * q * mean)).astype(
                    jnp.bfloat16
                )
                return carry

            lax.fori_loop(0, count // ROWS, rows, 0, unroll=2)
            copy = pltpu.make_async_copy(
                obuf.at[b, pl.ds(first, count)],
                out_hbm.at[0, b, pl.ds(first, count)],
                osem.at[0 if first == 0 else 1, b],
            )
            copy.start()
            out_copies.append(copy)

    head_backward(grad_query, 0, QLEN)

    for slot in range(1, n):
        place = lse_buf.at[slot]
        remote(place, place, lsend.at[slot], lrecv.at[slot], "dp", right).wait_recv()
    parts = [lse_buf[0]] + [pltpu.roll(lse_buf[k], k, 0) for k in range(1, n)]
    high = functools.reduce(jnp.maximum, parts)
    totals = high + jnp.log(sum(jnp.exp(part - high) for part in parts))
    for slot in range(n):
        rows = slice(slot * pairs, (slot + 1) * pairs)
        share = jnp.exp(smooth_all[rows, :] - totals[slot : slot + 1])
        slope = OBJECTIVE_FACTOR * sharp * (share - label_all[rows, :])
        tinv_all[rows, :] = weight_all[rows, :] * slope * tinv_all[rows, :]
    grad_doc = jnp.zeros((pairs * DLEN, docs.shape[2]), jnp.float32)
    for slot in range(n):
        grads(slot, e_all, tinv_all)
        grad_doc = grad_doc + dot(gbuf[slot], queries[slot], ((1,), (0,)))
    head_backward(grad_doc, QLEN, DLEN)

    for copy in started:
        copy.wait_send()
    for copy in out_copies:
        copy.wait()


def local(
    n,
    sections,
    latent_states,
    rescale_factor,
    embedding_matrix,
    request_span,
    passage_span,
    matching_pair,
    steepness_pair,
):
    _, pairs, length, width = latent_states.shape
    depth, features = embedding_matrix.shape
    rows = pairs * length
    lanes = pairs * QLEN
    f32, bf16 = jnp.float32, jnp.bfloat16
    dma = pltpu.SemaphoreType.DMA
    vmem = pl.BlockSpec(memory_space=pltpu.VMEM)
    smem = pl.BlockSpec(memory_space=pltpu.SMEM)
    anywhere = pl.BlockSpec(memory_space=pl.ANY)
    chips = sections // 2
    return pl.pallas_call(
        functools.partial(body, n, sections),
        out_shape=(
            jax.ShapeDtypeStruct(latent_states.shape, bf16),
            jax.ShapeDtypeStruct((1, pairs), f32),
        ),
        in_specs=[anywhere, vmem, anywhere, smem, smem, smem, smem],
        out_specs=(anywhere, vmem),
        scratch_shapes=[
            pltpu.VMEM((pairs, length, width), bf16),
            pltpu.VMEM((sections, rows, depth), bf16),
            pltpu.VMEM((sections, depth, features), bf16),
            pltpu.VMEM((rows, features), f32),
            pltpu.VMEM((rows, 128), f32),
            pltpu.VMEM((rows, features), f32),
            pltpu.VMEM((n, pairs * DLEN, features), bf16),
            pltpu.VMEM((n, pairs * QLEN, features), bf16),
            pltpu.VMEM((n, pairs * DLEN, lanes), f32),
            pltpu.VMEM((n, pairs * DLEN, lanes), f32),
            pltpu.VMEM((n, pairs * DLEN, lanes), bf16),
            pltpu.VMEM((pairs * DLEN, features), bf16),
            pltpu.VMEM((pairs * DLEN, width), f32),
            pltpu.VMEM((pairs, length, width), bf16),
            pltpu.VMEM((n * pairs, lanes), f32),
            pltpu.VMEM((n * pairs, lanes), f32),
            pltpu.VMEM((n * pairs, lanes), f32),
            pltpu.VMEM((n * pairs, lanes), f32),
            pltpu.VMEM((n * pairs, lanes), f32),
            pltpu.VMEM((n * pairs, lanes), f32),
            pltpu.VMEM((n * pairs, lanes), f32),
            pltpu.VMEM((n, n, lanes), f32),
            dma((pairs,)),
            dma(()),
            dma((2 * chips, CHUNKS)),
            dma((2 * chips, CHUNKS)),
            dma((2, n, DOC_CHUNKS)),
            dma((n, DOC_CHUNKS)),
            dma((2, n, QUERY_CHUNKS)),
            dma((n, QUERY_CHUNKS)),
            dma((n,)),
            dma((n,)),
            dma((2, pairs)),
        ],
        compiler_params=pltpu.CompilerParams(
            collective_id=0, has_side_effects=True, vmem_limit_bytes=60 * 1024 * 1024
        ),
        name="late_interaction",
    )(
        latent_states,
        rescale_factor.reshape(1, width),
        embedding_matrix,
        request_span,
        passage_span,
        matching_pair,
        steepness_pair,
    )


def solution(mesh):
    return jax.shard_map(
        functools.partial(local, mesh.shape["dp"], mesh.shape["section"]),
        mesh=mesh,
        in_specs=(P("section", "dp", None, None), P(), P("section", None), P(), P(), P(), P()),
        out_specs=(P("section", "dp", None, None), P("section", "dp")),
        check_vma=False,
    )
```

```python
import functools

import jax
import jax.numpy as jnp
from jax import lax
from jax.experimental import pallas as pl
from jax.experimental.pallas import tpu as pltpu
from jax.sharding import PartitionSpec as P

QLEN = 32
DLEN = 64

EPSILON = 1e-06
OBJECTIVE_FACTOR = 1024.0
MASKED = -1e30

ROWS = 16
CHUNKS = 2
QUERY_CHUNKS = 1
DOC_CHUNKS = 1


def dot(a, b, dims, precision=None):
    return lax.dot_general(
        a, b, (dims, ((), ())), precision=precision, preferred_element_type=jnp.float32
    )


def body(
    n,
    sections,
    x_hbm,
    gain_ref,
    w_hbm,
    request_ref,
    passage_ref,
    match_ref,
    steep_ref,
    gp_ref,
    w_all,
    loss_ref,
    xbuf,
    nrm,
    wbuf,
    proj,
    rinv,
    docs,
    queries,
    e_own,
    e_all,
    gbuf,
    smooth_own,
    tinv_own,
    smooth_all,
    tinv_all,
    label_own,
    label_all,
    weight_all,
    lse_buf,
    x_sem,
    w_sem,
    wsend,
    wrecv,
    dsend,
    drecv,
    qsend,
    qrecv,
    lsend,
    lrecv,
):
    pairs, length, width = xbuf.shape
    depth = wbuf.shape[1]
    lanes = pairs * QLEN
    section = lax.axis_index("section")
    me = lax.axis_index("dp")

    half = n // 2
    col = me % 2
    pos = (me // 2) * (1 - col) + (n - 1 - me // 2) * col

    def device_at(p):
        side = p // half
        return 2 * (p * (1 - side) + (n - 1 - p) * side) + side

    def owner_of(slot):
        return device_at((pos + n - slot) % n)

    right = device_at((pos + 1) % n)
    left = device_at((pos + n - 1) % n)

    chips = sections // 2
    core = section % 2
    chip = section // 2
    partner = chip * 2 + 1 - core

    def over(t):
        return ((chip + t) % chips) * 2 + core

    def remote(src, dst, send, recv, axis, index):
        return pltpu.make_async_remote_copy(
            src_ref=src,
            dst_ref=dst,
            send_sem=send,
            recv_sem=recv,
            device_id={axis: index},
            device_id_type=pl.DeviceIdType.MESH,
        )

    x_copies = [
        pltpu.make_async_copy(x_hbm.at[0, b], xbuf.at[b], x_sem.at[b]) for b in range(pairs)
    ]
    w_copy = pltpu.make_async_copy(w_hbm, wbuf.at[section], w_sem)
    w_copy.start()
    for copy in x_copies:
        copy.start()

    barrier = pltpu.get_barrier_semaphore()
    greeted = [("section", partner)]
    greeted += [("section", over(t)) for t in range(1, chips)]
    greeted += [("dp", right), ("dp", left)]
    for axis, index in greeted:
        pl.semaphore_signal(
            barrier, inc=1, device_id={axis: index}, device_id_type=pl.DeviceIdType.MESH
        )
    pl.semaphore_wait(barrier, len(greeted))

    part = depth // CHUNKS
    started = []

    def launch(copy):
        copy.start()
        started.append(copy)

    def piece(ref, index, h):
        return ref.at[index, pl.ds(h * part, part)]

    for t in range(1, chips):
        for h in range(CHUNKS):
            launch(
                remote(
                    w_hbm.at[pl.ds(h * part, part)],
                    piece(wbuf, section, h),
                    wsend.at[t, h],
                    wrecv.at[t, h],
                    "section",
                    over(t),
                )
            )
    for h in range(CHUNKS):
        launch(
            remote(
                w_hbm.at[pl.ds(h * part, part)],
                piece(wbuf, section, h),
                wsend.at[0, h],
                wrecv.at[0, h],
                "section",
                partner,
            )
        )

    gain = gain_ref[...]
    for b in range(pairs):
        x_copies[b].wait()

        def norm_rows(i, carry, b=b):
            r = pl.multiple_of(i * ROWS, ROWS)
            v = xbuf[b, pl.ds(r, ROWS), :].astype(jnp.float32)
            q = lax.rsqrt(jnp.sum(v * v, axis=1, keepdims=True) * (1.0 / width) + EPSILON)
            full = pl.multiple_of(b * length + i * ROWS, ROWS)
            z = (v * q * gain).astype(jnp.bfloat16)
            for k in range(sections):
                nrm[k, pl.ds(full, ROWS), :] = z[:, k * depth : (k + 1) * depth]
            return carry

        lax.fori_loop(0, length // ROWS, norm_rows, 0, unroll=2)

    def add_piece(index, first=False):
        term = dot(nrm[index], wbuf[index], ((1,), (0,)))
        proj[...] = term if first else proj[...] + term

    w_copy.wait()
    add_piece(section, True)
    for h in range(CHUNKS):
        place = piece(wbuf, partner, h)
        remote(place, place, wsend.at[0, h], wrecv.at[0, h], "section", partner).wait_recv()
    add_piece(partner)
    for t in range(1, chips):
        source = over(chips - t)
        for h in range(CHUNKS):
            place = piece(wbuf, source, h)
            remote(place, place, wsend.at[t, h], wrecv.at[t, h], "section", partner).wait_recv()
            launch(
                remote(
                    place,
                    place,
                    wsend.at[chips + t, h],
                    wrecv.at[chips + t, h],
                    "section",
                    partner,
                )
            )
        add_piece(source)
    for t in range(1, chips):
        source = ((chip + chips - t) % chips) * 2 + 1 - core
        for h in range(CHUNKS):
            place = piece(wbuf, source, h)
            remote(
                place, place, wsend.at[chips + t, h], wrecv.at[chips + t, h], "section", partner
            ).wait_recv()
        add_piece(source)

    w_out = pltpu.make_async_copy(wbuf, w_all, w_sem)
    w_out.start()

    for b in range(pairs):
        p = proj[b * length : (b + 1) * length, :]
        r = lax.rsqrt(jnp.sum(p * p, axis=1, keepdims=True) + EPSILON)
        rinv[b * length : (b + 1) * length, :] = jnp.broadcast_to(r, p.shape)
        v = (p * r).astype(jnp.bfloat16)
        queries[0, b * QLEN : (b + 1) * QLEN, :] = v[:QLEN]
        docs[0, b * DLEN : (b + 1) * DLEN, :] = v[QLEN:]

    def chunk(buf, slot, h, count):
        size = buf.shape[1] // count
        return buf.at[slot, pl.ds(h * size, size)]

    def onward(chain, slot, h):
        buf, send, recv, ascending, _, count = chain
        to = slot + 1 if ascending else (n if slot == 0 else slot) - 1
        return remote(
            chunk(buf, slot, h, count),
            chunk(buf, to, h, count),
            send.at[0 if ascending else 1, slot, h],
            recv.at[to, h],
            "dp",
            right if ascending else left,
        )

    query_chains = [
        (queries, qsend, qrecv, True, n // 2, QUERY_CHUNKS),
        (queries, qsend, qrecv, False, n - 1 - n // 2, QUERY_CHUNKS),
    ]
    doc_chains = [
        (docs, dsend, drecv, True, n - 1 - n // 2, DOC_CHUNKS),
        (docs, dsend, drecv, False, n // 2, DOC_CHUNKS),
    ]

    def pass_on(chains, d):
        for h in range(chains[0][5]):
            for chain in chains:
                buf, send, recv, ascending, reach, count = chain
                if d > 0 and reach >= d:
                    slot = d if ascending else n - d
                    place = chunk(buf, slot, h, count)
                    remote(
                        place, place, send.at[0, 0, h], recv.at[slot, h], "dp", right
                    ).wait_recv()
                if reach > d:
                    launch(onward(chain, d if ascending else (n - d) % n, h))

    pass_on(query_chains, 0)
    pass_on(doc_chains, 0)

    beta = steep_ref[0]
    sharp = steep_ref[1]
    inverse_beta = 1.0 / jnp.full((1, lanes), beta, jnp.float32)
    place_j = lax.broadcasted_iota(jnp.int32, (DLEN, lanes), 0)
    lane = lax.broadcasted_iota(jnp.int32, (1, lanes), 1)
    lane_pair = lane // QLEN
    lane_token = lane % QLEN

    def spread(ref, first):
        value = jnp.full((1, lanes), ref[section, first], jnp.int32)
        for b in range(1, pairs):
            value = jnp.where(lane_pair == b, ref[section, first + b], value)
        return value

    def weights_of(owner):
        span = spread(request_ref, owner * pairs)
        return jnp.where(lane_token < span, 1.0 / span.astype(jnp.float32), 0.0)

    def forward(doc_rows, query_rows, owner, slot, e_ref, smooth_ref, tinv_ref):
        s = dot(doc_rows, query_rows, ((1,), (1,)))
        for c in range(pairs):
            span = passage_ref[section, owner * pairs + c]
            sc = jnp.where(place_j < span, beta * s[c * DLEN : (c + 1) * DLEN], MASKED)
            high = jnp.max(sc, axis=0, keepdims=True)
            e = jnp.exp(sc - high)
            total = jnp.sum(e, axis=0, keepdims=True)
            e_ref[slot, c * DLEN : (c + 1) * DLEN, :] = e
            row = slot * pairs + c
            smooth_ref[row : row + 1, :] = (high + jnp.log(total)) * inverse_beta
            tinv_ref[row : row + 1, :] = 1.0 / total

    own_weight = weights_of(me)
    own_match = spread(match_ref, me * pairs)

    def own_forward(slot):
        owner = owner_of(slot)
        forward(docs[slot], queries[0], owner, slot, e_own, smooth_own, tinv_own)
        for c in range(pairs):
            row = slot * pairs + c
            label_own[row : row + 1, :] = jnp.where(own_match == owner * pairs + c, 1.0, 0.0)

    def doc_forward(slot):
        forward(docs[0], queries[slot], me, slot, e_all, smooth_all, tinv_all)

    doc_forward(0)
    own_forward(0)
    for slot in range(n):
        owner = owner_of(slot)
        match = spread(match_ref, owner * pairs)
        weight = weights_of(owner)
        for c in range(pairs):
            row = slot * pairs + c
            label_all[row : row + 1, :] = jnp.where(match == me * pairs + c, 1.0, 0.0)
            weight_all[row : row + 1, :] = weight

    from_lane = lax.broadcasted_iota(jnp.int32, (lanes, lanes), 0) // QLEN
    to_lane = lax.broadcasted_iota(jnp.int32, (lanes, lanes), 1) // QLEN
    same = jnp.where(from_lane == to_lane, 1.0, 0.0)
    highest = lax.Precision.HIGHEST

    for d in range(1, n // 2 + 1):
        pass_on(query_chains, d)
        for slot in sorted({d, n - d}):
            doc_forward(slot)
        if d == n // 2:
            smooth_all[...] = sharp * dot(
                smooth_all[...] * weight_all[...], same, ((1,), (0,)), highest
            )
            for slot in range(n):
                logits = smooth_all[slot * pairs : (slot + 1) * pairs, :]
                high = jnp.max(logits, axis=0, keepdims=True)
                lse_buf[0, slot : slot + 1, :] = high + jnp.log(
                    jnp.sum(jnp.exp(logits - high), axis=0, keepdims=True)
                )
            for k in range(1, n):
                launch(
                    remote(
                        lse_buf.at[0],
                        lse_buf.at[k],
                        lsend.at[k],
                        lrecv.at[k],
                        "dp",
                        device_at((pos + k) % n),
                    )
                )
        pass_on(doc_chains, d)
        for slot in sorted({d, n - d}):
            own_forward(slot)

    scores = dot(smooth_own[...] * own_weight, same, ((1,), (0,)), highest)
    logits = sharp * scores
    high = jnp.max(logits, axis=0, keepdims=True)
    lse = high + jnp.log(jnp.sum(jnp.exp(logits - high), axis=0, keepdims=True))
    label = label_own[...]
    loss = lse - jnp.sum(logits * label, axis=0, keepdims=True)
    for b in range(pairs):
        loss_ref[:, b : b + 1] = loss[:, b * QLEN : b * QLEN + 1]
    slope = OBJECTIVE_FACTOR * sharp * (jnp.exp(logits - lse) - label)
    tinv_own[...] = own_weight * slope * tinv_own[...]

    def grads(slot, e_ref, coefficient_ref):
        for c in range(pairs):
            row = slot * pairs + c
            gbuf[slot, c * DLEN : (c + 1) * DLEN, :] = (
                coefficient_ref[row : row + 1, :] * e_ref[slot, c * DLEN : (c + 1) * DLEN, :]
            ).astype(jnp.bfloat16)

    for slot in range(n):
        grads(slot, e_own, tinv_own)
    grad_query = dot(
        gbuf[...].reshape(n * pairs * DLEN, lanes),
        docs[...].reshape(n * pairs * DLEN, docs.shape[2]),
        ((0,), (0,)),
    )

    def head_backward(gradient, first, count):
        for b in range(pairs):
            lo = b * length + first
            g = gradient[b * count : (b + 1) * count]
            r = rinv[lo : lo + count, :]
            u = proj[lo : lo + count, :] * r
            along = jnp.sum(u * g, axis=1, keepdims=True)
            gp_ref[lo : lo + count, :] = (r * (g - u * along)).astype(jnp.bfloat16)

    head_backward(grad_query, 0, QLEN)

    for slot in range(1, n):
        place = lse_buf.at[slot]
        remote(place, place, lsend.at[slot], lrecv.at[slot], "dp", right).wait_recv()
    parts = [lse_buf[0]] + [pltpu.roll(lse_buf[k], k, 0) for k in range(1, n)]
    high = functools.reduce(jnp.maximum, parts)
    totals = high + jnp.log(sum(jnp.exp(part - high) for part in parts))
    for slot in range(n):
        rows = slice(slot * pairs, (slot + 1) * pairs)
        share = jnp.exp(smooth_all[rows, :] - totals[slot : slot + 1])
        slope = OBJECTIVE_FACTOR * sharp * (share - label_all[rows, :])
        tinv_all[rows, :] = weight_all[rows, :] * slope * tinv_all[rows, :]
    grad_doc = jnp.zeros((pairs * DLEN, docs.shape[2]), jnp.float32)
    for slot in range(n):
        grads(slot, e_all, tinv_all)
        grad_doc = grad_doc + dot(gbuf[slot], queries[slot], ((1,), (0,)))
    head_backward(grad_doc, QLEN, DLEN)

    for copy in started:
        copy.wait_send()
    w_out.wait()


def last_body(x_ref, gain_ref, w_ref, gp_ref, loss_in, out_ref, loss_ref, gnbuf):
    _, _, length, width = x_ref.shape
    sections, depth, features = w_ref.shape
    gain = gain_ref[...]
    all_w = w_ref[...].reshape(sections * depth, features)
    gnbuf[...] = dot(gp_ref[...], all_w, ((1,), (1,)))
    loss_ref[...] = loss_in[...]

    def rows(i, carry):
        r = pl.multiple_of(i * ROWS, ROWS)
        v = x_ref[0, 0, pl.ds(r, ROWS), :].astype(jnp.float32)
        weighted = gnbuf[pl.ds(r, ROWS), :] * gain
        mean = jnp.sum(v * weighted, axis=1, keepdims=True) * (1.0 / width)
        q = lax.rsqrt(jnp.sum(v * v, axis=1, keepdims=True) * (1.0 / width) + EPSILON)
        out_ref[0, 0, pl.ds(r, ROWS), :] = (q * weighted - v * (q * q * q * mean)).astype(
            jnp.bfloat16
        )
        return carry

    lax.fori_loop(0, length // ROWS, rows, 0, unroll=True)


def local(
    n,
    sections,
    latent_states,
    rescale_factor,
    embedding_matrix,
    request_span,
    passage_span,
    matching_pair,
    steepness_pair,
):
    _, pairs, length, width = latent_states.shape
    depth, features = embedding_matrix.shape
    rows = pairs * length
    lanes = pairs * QLEN
    f32, bf16 = jnp.float32, jnp.bfloat16
    dma = pltpu.SemaphoreType.DMA
    vmem = pl.BlockSpec(memory_space=pltpu.VMEM)
    smem = pl.BlockSpec(memory_space=pltpu.SMEM)
    anywhere = pl.BlockSpec(memory_space=pl.ANY)
    chips = sections // 2
    gain = rescale_factor.reshape(1, width)
    grad_projected, whole_w, loss = pl.pallas_call(
        functools.partial(body, n, sections),
        out_shape=(
            jax.ShapeDtypeStruct((rows, features), bf16),
            jax.ShapeDtypeStruct((sections, depth, features), bf16),
            jax.ShapeDtypeStruct((1, pairs), f32),
        ),
        in_specs=[anywhere, vmem, anywhere, smem, smem, smem, smem],
        out_specs=(vmem, anywhere, vmem),
        scratch_shapes=[
            pltpu.VMEM((pairs, length, width), bf16),
            pltpu.VMEM((sections, rows, depth), bf16),
            pltpu.VMEM((sections, depth, features), bf16),
            pltpu.VMEM((rows, features), f32),
            pltpu.VMEM((rows, features), f32),
            pltpu.VMEM((n, pairs * DLEN, features), bf16),
            pltpu.VMEM((n, pairs * QLEN, features), bf16),
            pltpu.VMEM((n, pairs * DLEN, lanes), f32),
            pltpu.VMEM((n, pairs * DLEN, lanes), f32),
            pltpu.VMEM((n, pairs * DLEN, lanes), bf16),
            pltpu.VMEM((n * pairs, lanes), f32),
            pltpu.VMEM((n * pairs, lanes), f32),
            pltpu.VMEM((n * pairs, lanes), f32),
            pltpu.VMEM((n * pairs, lanes), f32),
            pltpu.VMEM((n * pairs, lanes), f32),
            pltpu.VMEM((n * pairs, lanes), f32),
            pltpu.VMEM((n * pairs, lanes), f32),
            pltpu.VMEM((n, n, lanes), f32),
            dma((pairs,)),
            dma(()),
            dma((2 * chips, CHUNKS)),
            dma((2 * chips, CHUNKS)),
            dma((2, n, DOC_CHUNKS)),
            dma((n, DOC_CHUNKS)),
            dma((2, n, QUERY_CHUNKS)),
            dma((n, QUERY_CHUNKS)),
            dma((n,)),
            dma((n,)),
                ],
        compiler_params=pltpu.CompilerParams(
            collective_id=0, has_side_effects=True, vmem_limit_bytes=60 * 1024 * 1024
        ),
        name="late_interaction",
    )(
        latent_states,
        gain,
        embedding_matrix,
        request_span,
        passage_span,
        matching_pair,
        steepness_pair,
    )
    tokens = pl.BlockSpec((1, 1, length, width), lambda b: (0, b, 0, 0))
    losses = pl.BlockSpec((1, pairs), lambda b: (0, 0))
    return pl.pallas_call(
        last_body,
        grid=(pairs,),
        out_shape=(
            jax.ShapeDtypeStruct(latent_states.shape, bf16),
            jax.ShapeDtypeStruct((1, pairs), f32),
        ),
        in_specs=[
            tokens,
            pl.BlockSpec((1, width), lambda b: (0, 0)),
            pl.BlockSpec((sections, depth, features), lambda b: (0, 0, 0)),
            pl.BlockSpec((length, features), lambda b: (b, 0)),
            losses,
        ],
        out_specs=(tokens, losses),
        scratch_shapes=[pltpu.VMEM((length, width), f32)],
        compiler_params=pltpu.CompilerParams(vmem_limit_bytes=24 * 1024 * 1024),
        name="head_backward",
    )(latent_states, gain, whole_w, grad_projected, loss)


def solution(mesh):
    return jax.shard_map(
        functools.partial(local, mesh.shape["dp"], mesh.shape["section"]),
        mesh=mesh,
        in_specs=(P("section", "dp", None, None), P(), P("section", None), P(), P(), P(), P()),
        out_specs=(P("section", "dp", None, None), P("section", "dp")),
        check_vma=False,
    )
```

```python
import functools

import jax
import jax.numpy as jnp
from jax import lax
from jax.experimental import pallas as pl
from jax.experimental.pallas import tpu as pltpu
from jax.sharding import PartitionSpec as P

QLEN = 32
DLEN = 64

EPSILON = 1e-06
OBJECTIVE_FACTOR = 1024.0
MASKED = -1e30

ROWS = 16
CHUNKS = 2
QUERY_CHUNKS = 1
DOC_CHUNKS = 1


def dot(a, b, dims, precision=None):
    return lax.dot_general(
        a, b, (dims, ((), ())), precision=precision, preferred_element_type=jnp.float32
    )


def body(
    n,
    sections,
    x_hbm,
    gain_ref,
    w_hbm,
    request_ref,
    passage_ref,
    match_ref,
    steep_ref,
    gp_ref,
    w_all,
    loss_ref,
    xbuf,
    nrm,
    wbuf,
    proj,
    rinv,
    docs,
    queries,
    e_own,
    e_all,
    gbuf,
    smooth_own,
    tinv_own,
    smooth_all,
    tinv_all,
    label_own,
    label_all,
    weight_all,
    lse_buf,
    x_sem,
    w_sem,
    wsend,
    wrecv,
    dsend,
    drecv,
    qsend,
    qrecv,
    lsend,
    lrecv,
):
    pairs, length, width = xbuf.shape
    depth = wbuf.shape[1]
    lanes = pairs * QLEN
    section = lax.axis_index("section")
    me = lax.axis_index("dp")

    half = n // 2
    col = me % 2
    pos = (me // 2) * (1 - col) + (n - 1 - me // 2) * col

    def device_at(p):
        side = p // half
        return 2 * (p * (1 - side) + (n - 1 - p) * side) + side

    def owner_of(slot):
        return device_at((pos + n - slot) % n)

    right = device_at((pos + 1) % n)
    left = device_at((pos + n - 1) % n)

    chips = sections // 2
    core = section % 2
    chip = section // 2
    partner = chip * 2 + 1 - core

    def over(t):
        return ((chip + t) % chips) * 2 + core

    def remote(src, dst, send, recv, axis, index):
        return pltpu.make_async_remote_copy(
            src_ref=src,
            dst_ref=dst,
            send_sem=send,
            recv_sem=recv,
            device_id={axis: index},
            device_id_type=pl.DeviceIdType.MESH,
        )

    x_copies = [
        pltpu.make_async_copy(x_hbm.at[0, b], xbuf.at[b], x_sem.at[b]) for b in range(pairs)
    ]
    w_copy = pltpu.make_async_copy(w_hbm, wbuf.at[section], w_sem)
    w_copy.start()
    for copy in x_copies:
        copy.start()

    barrier = pltpu.get_barrier_semaphore()
    greeted = [("section", partner)]
    greeted += [("section", over(t)) for t in range(1, chips)]
    greeted += [("dp", right), ("dp", left)]
    for axis, index in greeted:
        pl.semaphore_signal(
            barrier, inc=1, device_id={axis: index}, device_id_type=pl.DeviceIdType.MESH
        )
    pl.semaphore_wait(barrier, len(greeted))

    part = depth // CHUNKS
    started = []

    def launch(copy):
        copy.start()
        started.append(copy)

    def piece(ref, index, h):
        return ref.at[index, pl.ds(h * part, part)]

    for t in range(1, chips):
        for h in range(CHUNKS):
            launch(
                remote(
                    w_hbm.at[pl.ds(h * part, part)],
                    piece(wbuf, section, h),
                    wsend.at[t, h],
                    wrecv.at[t, h],
                    "section",
                    over(t),
                )
            )
    for h in range(CHUNKS):
        launch(
            remote(
                w_hbm.at[pl.ds(h * part, part)],
                piece(wbuf, section, h),
                wsend.at[0, h],
                wrecv.at[0, h],
                "section",
                partner,
            )
        )

    gain = gain_ref[...]
    for b in range(pairs):
        x_copies[b].wait()

        def norm_rows(i, carry, b=b):
            r = pl.multiple_of(i * ROWS, ROWS)
            v = xbuf[b, pl.ds(r, ROWS), :].astype(jnp.float32)
            q = lax.rsqrt(jnp.sum(v * v, axis=1, keepdims=True) * (1.0 / width) + EPSILON)
            full = pl.multiple_of(b * length + i * ROWS, ROWS)
            z = (v * q * gain).astype(jnp.bfloat16)
            for k in range(sections):
                nrm[k, pl.ds(full, ROWS), :] = z[:, k * depth : (k + 1) * depth]
            return carry

        lax.fori_loop(0, length // ROWS, norm_rows, 0, unroll=2)

    def add_piece(index, first=False):
        term = dot(nrm[index], wbuf[index], ((1,), (0,)))
        proj[...] = term if first else proj[...] + term

    w_copy.wait()
    add_piece(section, True)
    for h in range(CHUNKS):
        place = piece(wbuf, partner, h)
        remote(place, place, wsend.at[0, h], wrecv.at[0, h], "section", partner).wait_recv()
    add_piece(partner)
    for t in range(1, chips):
        source = over(chips - t)
        for h in range(CHUNKS):
            place = piece(wbuf, source, h)
            remote(place, place, wsend.at[t, h], wrecv.at[t, h], "section", partner).wait_recv()
            launch(
                remote(
                    place,
                    place,
                    wsend.at[chips + t, h],
                    wrecv.at[chips + t, h],
                    "section",
                    partner,
                )
            )
        add_piece(source)
    for t in range(1, chips):
        source = ((chip + chips - t) % chips) * 2 + 1 - core
        for h in range(CHUNKS):
            place = piece(wbuf, source, h)
            remote(
                place, place, wsend.at[chips + t, h], wrecv.at[chips + t, h], "section", partner
            ).wait_recv()
        add_piece(source)

    w_out = pltpu.make_async_copy(wbuf, w_all, w_sem)
    w_out.start()

    for b in range(pairs):
        p = proj[b * length : (b + 1) * length, :]
        r = lax.rsqrt(jnp.sum(p * p, axis=1, keepdims=True) + EPSILON)
        rinv[b * length : (b + 1) * length, :] = jnp.broadcast_to(r, p.shape)
        v = (p * r).astype(jnp.bfloat16)
        queries[0, b * QLEN : (b + 1) * QLEN, :] = v[:QLEN]
        docs[0, b * DLEN : (b + 1) * DLEN, :] = v[QLEN:]

    def chunk(buf, slot, h, count):
        size = buf.shape[1] // count
        return buf.at[slot, pl.ds(h * size, size)]

    def onward(chain, slot, h):
        buf, send, recv, ascending, _, count = chain
        to = slot + 1 if ascending else (n if slot == 0 else slot) - 1
        return remote(
            chunk(buf, slot, h, count),
            chunk(buf, to, h, count),
            send.at[0 if ascending else 1, slot, h],
            recv.at[to, h],
            "dp",
            right if ascending else left,
        )

    query_chains = [
        (queries, qsend, qrecv, True, n // 2, QUERY_CHUNKS),
        (queries, qsend, qrecv, False, n - 1 - n // 2, QUERY_CHUNKS),
    ]
    doc_chains = [
        (docs, dsend, drecv, True, n - 1 - n // 2, DOC_CHUNKS),
        (docs, dsend, drecv, False, n // 2, DOC_CHUNKS),
    ]

    def pass_on(chains, d):
        for h in range(chains[0][5]):
            for chain in chains:
                buf, send, recv, ascending, reach, count = chain
                if d > 0 and reach >= d:
                    slot = d if ascending else n - d
                    place = chunk(buf, slot, h, count)
                    remote(
                        place, place, send.at[0, 0, h], recv.at[slot, h], "dp", right
                    ).wait_recv()
                if reach > d:
                    launch(onward(chain, d if ascending else (n - d) % n, h))

    pass_on(query_chains, 0)
    pass_on(doc_chains, 0)

    beta = steep_ref[0]
    sharp = steep_ref[1]
    inverse_beta = 1.0 / jnp.full((1, lanes), beta, jnp.float32)
    place_j = lax.broadcasted_iota(jnp.int32, (DLEN, lanes), 0)
    lane = lax.broadcasted_iota(jnp.int32, (1, lanes), 1)
    lane_pair = lane // QLEN
    lane_token = lane % QLEN

    def spread(ref, first):
        value = jnp.full((1, lanes), ref[section, first], jnp.int32)
        for b in range(1, pairs):
            value = jnp.where(lane_pair == b, ref[section, first + b], value)
        return value

    def weights_of(owner):
        span = spread(request_ref, owner * pairs)
        return jnp.where(lane_token < span, 1.0 / span.astype(jnp.float32), 0.0)

    def forward(doc_rows, query_rows, owner, slot, e_ref, smooth_ref, tinv_ref):
        s = dot(doc_rows, query_rows, ((1,), (1,)))
        for c in range(pairs):
            span = passage_ref[section, owner * pairs + c]
            sc = jnp.where(place_j < span, beta * s[c * DLEN : (c + 1) * DLEN], MASKED)
            high = jnp.max(sc, axis=0, keepdims=True)
            e = jnp.exp(sc - high)
            total = jnp.sum(e, axis=0, keepdims=True)
            e_ref[slot, c * DLEN : (c + 1) * DLEN, :] = e
            row = slot * pairs + c
            smooth_ref[row : row + 1, :] = (high + jnp.log(total)) * inverse_beta
            tinv_ref[row : row + 1, :] = 1.0 / total

    own_weight = weights_of(me)
    own_match = spread(match_ref, me * pairs)

    def own_forward(slot):
        owner = owner_of(slot)
        forward(docs[slot], queries[0], owner, slot, e_own, smooth_own, tinv_own)
        for c in range(pairs):
            row = slot * pairs + c
            label_own[row : row + 1, :] = jnp.where(own_match == owner * pairs + c, 1.0, 0.0)

    def doc_forward(slot):
        forward(docs[0], queries[slot], me, slot, e_all, smooth_all, tinv_all)

    doc_forward(0)
    own_forward(0)
    for slot in range(n):
        owner = owner_of(slot)
        match = spread(match_ref, owner * pairs)
        weight = weights_of(owner)
        for c in range(pairs):
            row = slot * pairs + c
            label_all[row : row + 1, :] = jnp.where(match == me * pairs + c, 1.0, 0.0)
            weight_all[row : row + 1, :] = weight

    from_lane = lax.broadcasted_iota(jnp.int32, (lanes, lanes), 0) // QLEN
    to_lane = lax.broadcasted_iota(jnp.int32, (lanes, lanes), 1) // QLEN
    same = jnp.where(from_lane == to_lane, 1.0, 0.0)
    highest = lax.Precision.HIGHEST

    for d in range(1, n // 2 + 1):
        pass_on(query_chains, d)
        for slot in sorted({d, n - d}):
            doc_forward(slot)
        if d == n // 2:
            smooth_all[...] = sharp * dot(
                smooth_all[...] * weight_all[...], same, ((1,), (0,)), highest
            )
            for slot in range(n):
                logits = smooth_all[slot * pairs : (slot + 1) * pairs, :]
                high = jnp.max(logits, axis=0, keepdims=True)
                lse_buf[0, slot : slot + 1, :] = high + jnp.log(
                    jnp.sum(jnp.exp(logits - high), axis=0, keepdims=True)
                )
            for k in range(1, n):
                launch(
                    remote(
                        lse_buf.at[0],
                        lse_buf.at[k],
                        lsend.at[k],
                        lrecv.at[k],
                        "dp",
                        device_at((pos + k) % n),
                    )
                )
        pass_on(doc_chains, d)
        for slot in sorted({d, n - d}):
            own_forward(slot)

    scores = dot(smooth_own[...] * own_weight, same, ((1,), (0,)), highest)
    logits = sharp * scores
    high = jnp.max(logits, axis=0, keepdims=True)
    lse = high + jnp.log(jnp.sum(jnp.exp(logits - high), axis=0, keepdims=True))
    label = label_own[...]
    loss = lse - jnp.sum(logits * label, axis=0, keepdims=True)
    for b in range(pairs):
        loss_ref[:, b : b + 1] = loss[:, b * QLEN : b * QLEN + 1]
    slope = OBJECTIVE_FACTOR * sharp * (jnp.exp(logits - lse) - label)
    tinv_own[...] = own_weight * slope * tinv_own[...]

    def grads(slot, e_ref, coefficient_ref):
        for c in range(pairs):
            row = slot * pairs + c
            gbuf[slot, c * DLEN : (c + 1) * DLEN, :] = (
                coefficient_ref[row : row + 1, :] * e_ref[slot, c * DLEN : (c + 1) * DLEN, :]
            ).astype(jnp.bfloat16)

    for slot in range(n):
        grads(slot, e_own, tinv_own)
    grad_query = dot(
        gbuf[...].reshape(n * pairs * DLEN, lanes),
        docs[...].reshape(n * pairs * DLEN, docs.shape[2]),
        ((0,), (0,)),
    )

    def head_backward(gradient, first, count):
        for b in range(pairs):
            lo = b * length + first
            g = gradient[b * count : (b + 1) * count]
            r = rinv[lo : lo + count, :]
            u = proj[lo : lo + count, :] * r
            along = jnp.sum(u * g, axis=1, keepdims=True)
            gp_ref[lo : lo + count, :] = (r * (g - u * along)).astype(jnp.bfloat16)

    head_backward(grad_query, 0, QLEN)

    for slot in range(1, n):
        place = lse_buf.at[slot]
        remote(place, place, lsend.at[slot], lrecv.at[slot], "dp", right).wait_recv()
    parts = [lse_buf[0]] + [pltpu.roll(lse_buf[k], k, 0) for k in range(1, n)]
    high = functools.reduce(jnp.maximum, parts)
    totals = high + jnp.log(sum(jnp.exp(part - high) for part in parts))
    for slot in range(n):
        rows = slice(slot * pairs, (slot + 1) * pairs)
        share = jnp.exp(smooth_all[rows, :] - totals[slot : slot + 1])
        slope = OBJECTIVE_FACTOR * sharp * (share - label_all[rows, :])
        tinv_all[rows, :] = weight_all[rows, :] * slope * tinv_all[rows, :]
    grad_doc = jnp.zeros((pairs * DLEN, docs.shape[2]), jnp.float32)
    for slot in range(n):
        grads(slot, e_all, tinv_all)
        grad_doc = grad_doc + dot(gbuf[slot], queries[slot], ((1,), (0,)))
    head_backward(grad_doc, QLEN, DLEN)

    for copy in started:
        copy.wait_send()
    w_out.wait()


def last_body(
    x_ref, gain_ref, w_hbm, gp_hbm, loss_hbm, out_ref, loss_ref, gnbuf, w_ref, gp_ref, loss_in, sem
):
    @pl.when(pl.program_id(0) == 0)
    def _():
        copies = [
            pltpu.make_async_copy(w_hbm, w_ref, sem.at[0]),
            pltpu.make_async_copy(gp_hbm, gp_ref, sem.at[1]),
            pltpu.make_async_copy(loss_hbm, loss_in, sem.at[2]),
        ]
        for copy in copies:
            copy.start()
        for copy in copies:
            copy.wait()

    _, _, length, width = x_ref.shape
    sections, depth, features = w_ref.shape
    gain = gain_ref[...]
    all_w = w_ref[...].reshape(sections * depth, features)
    first = pl.multiple_of(pl.program_id(0) * length, ROWS)
    gnbuf[...] = dot(gp_ref[pl.ds(first, length), :], all_w, ((1,), (1,)))
    loss_ref[...] = loss_in[...]

    def rows(i, carry):
        r = pl.multiple_of(i * ROWS, ROWS)
        v = x_ref[0, 0, pl.ds(r, ROWS), :].astype(jnp.float32)
        weighted = gnbuf[pl.ds(r, ROWS), :] * gain
        mean = jnp.sum(v * weighted, axis=1, keepdims=True) * (1.0 / width)
        q = lax.rsqrt(jnp.sum(v * v, axis=1, keepdims=True) * (1.0 / width) + EPSILON)
        out_ref[0, 0, pl.ds(r, ROWS), :] = (q * weighted - v * (q * q * q * mean)).astype(
            jnp.bfloat16
        )
        return carry

    lax.fori_loop(0, length // ROWS, rows, 0, unroll=True)


def local(
    n,
    sections,
    latent_states,
    rescale_factor,
    embedding_matrix,
    request_span,
    passage_span,
    matching_pair,
    steepness_pair,
):
    _, pairs, length, width = latent_states.shape
    depth, features = embedding_matrix.shape
    rows = pairs * length
    lanes = pairs * QLEN
    f32, bf16 = jnp.float32, jnp.bfloat16
    dma = pltpu.SemaphoreType.DMA
    vmem = pl.BlockSpec(memory_space=pltpu.VMEM)
    smem = pl.BlockSpec(memory_space=pltpu.SMEM)
    anywhere = pl.BlockSpec(memory_space=pl.ANY)
    chips = sections // 2
    gain = rescale_factor.reshape(1, width)
    grad_projected, whole_w, loss = pl.pallas_call(
        functools.partial(body, n, sections),
        out_shape=(
            jax.ShapeDtypeStruct((rows, features), bf16),
            jax.ShapeDtypeStruct((sections, depth, features), bf16),
            jax.ShapeDtypeStruct((1, pairs), f32),
        ),
        in_specs=[anywhere, vmem, anywhere, smem, smem, smem, smem],
        out_specs=(vmem, anywhere, vmem),
        scratch_shapes=[
            pltpu.VMEM((pairs, length, width), bf16),
            pltpu.VMEM((sections, rows, depth), bf16),
            pltpu.VMEM((sections, depth, features), bf16),
            pltpu.VMEM((rows, features), f32),
            pltpu.VMEM((rows, features), f32),
            pltpu.VMEM((n, pairs * DLEN, features), bf16),
            pltpu.VMEM((n, pairs * QLEN, features), bf16),
            pltpu.VMEM((n, pairs * DLEN, lanes), f32),
            pltpu.VMEM((n, pairs * DLEN, lanes), f32),
            pltpu.VMEM((n, pairs * DLEN, lanes), bf16),
            pltpu.VMEM((n * pairs, lanes), f32),
            pltpu.VMEM((n * pairs, lanes), f32),
            pltpu.VMEM((n * pairs, lanes), f32),
            pltpu.VMEM((n * pairs, lanes), f32),
            pltpu.VMEM((n * pairs, lanes), f32),
            pltpu.VMEM((n * pairs, lanes), f32),
            pltpu.VMEM((n * pairs, lanes), f32),
            pltpu.VMEM((n, n, lanes), f32),
            dma((pairs,)),
            dma(()),
            dma((2 * chips, CHUNKS)),
            dma((2 * chips, CHUNKS)),
            dma((2, n, DOC_CHUNKS)),
            dma((n, DOC_CHUNKS)),
            dma((2, n, QUERY_CHUNKS)),
            dma((n, QUERY_CHUNKS)),
            dma((n,)),
            dma((n,)),
                ],
        compiler_params=pltpu.CompilerParams(
            collective_id=0, has_side_effects=True, vmem_limit_bytes=60 * 1024 * 1024
        ),
        name="late_interaction",
    )(
        latent_states,
        gain,
        embedding_matrix,
        request_span,
        passage_span,
        matching_pair,
        steepness_pair,
    )
    tokens = pl.BlockSpec((1, 1, length, width), lambda b: (0, b, 0, 0))
    losses = pl.BlockSpec((1, pairs), lambda b: (0, 0))
    return pl.pallas_call(
        last_body,
        grid=(pairs,),
        out_shape=(
            jax.ShapeDtypeStruct(latent_states.shape, bf16),
            jax.ShapeDtypeStruct((1, pairs), f32),
        ),
        in_specs=[
            tokens,
            pl.BlockSpec((1, width), lambda b: (0, 0)),
            pl.BlockSpec(memory_space=pltpu.HBM),
            pl.BlockSpec(memory_space=pltpu.HBM),
            pl.BlockSpec(memory_space=pltpu.HBM),
        ],
        out_specs=(tokens, losses),
        scratch_shapes=[
            pltpu.VMEM((length, width), f32),
            pltpu.VMEM((sections, depth, features), bf16),
            pltpu.VMEM((rows, features), bf16),
            pltpu.VMEM((1, pairs), f32),
            dma((3,)),
        ],
        compiler_params=pltpu.CompilerParams(vmem_limit_bytes=67043328),
        name="head_backward",
    )(latent_states, gain, whole_w, grad_projected, loss)


def solution(mesh):
    return jax.shard_map(
        functools.partial(local, mesh.shape["dp"], mesh.shape["section"]),
        mesh=mesh,
        in_specs=(P("section", "dp", None, None), P(), P("section", None), P(), P(), P(), P()),
        out_specs=(P("section", "dp", None, None), P("section", "dp")),
        check_vma=False,
    )
```
